32 devices in a mesh: rep: 4 (over x, core), shard: 8 (over z, y).
Axes of the slice: x: 2, y: 2, z: 4, core: 2. Of those that a mesh axis runs over, the one named last changes fastest.
Arguments:
- inputs: bfloat16 [64, 750, 512], P(('rep', 'shard')), may hold values from -48 to 48
- cotangent: float32 [64, 750, 512], P(('rep', 'shard')), may hold values from -6 to 6
- row_weights: bfloat16 [512, 8192], P('shard'), may hold values from -1.41421356 to 1.41421356
- down_weights: bfloat16 [2, 2048, 512], P(None, 'shard'), may hold values from -0.125 to 0.125
- hidden_bias: bfloat16 [2, 2048], P(None, 'shard'), may hold values from -0.5 to 0.5
- vectors: bfloat16 [53, 512], P(None, 'shard'), may hold values from -1 to 2
- row_first: float32 [512, 8192], P('shard'), may hold values from -64 to 64
- down_first: float32 [2, 2048, 512], P(None, 'shard'), may hold values from -64 to 64
- hidden_first: float32 [2, 2048], P(None, 'shard'), may hold values from -64 to 64
- vector_first: float32 [53, 512], P(None, 'shard'), may hold values from -64 to 64
- row_second: float32 [512, 8192], P('shard'), may hold values from 24 to 240
- down_second: float32 [2, 2048, 512], P(None, 'shard'), may hold values from 24 to 240
- hidden_second: float32 [2, 2048], P(None, 'shard'), may hold values from 24 to 240
- vector_second: float32 [53, 512], P(None, 'shard'), may hold values from 24 to 240
- step_number: int32 [1], replicated, may hold values from 1 to 20
Outputs:
- outputs: float32 [64, 750, 512], P(('rep', 'shard'))
- input_grad: float32 [64, 750, 512], P(('rep', 'shard'))
- row_grad: float32 [512, 8192], P('shard')
- down_grad: float32 [2, 2048, 512], P(None, 'shard')
- hidden_grad: float32 [2, 2048], P(None, 'shard')
- vector_grad: float32 [53, 512], P(None, 'shard')
- row_first_new: float32 [512, 8192], P('shard')
- down_first_new: float32 [2, 2048, 512], P(None, 'shard')
- hidden_first_new: float32 [2, 2048], P(None, 'shard')
- vector_first_new: float32 [53, 512], P(None, 'shard')
- row_second_new: float32 [512, 8192], P('shard')
- down_second_new: float32 [2, 2048, 512], P(None, 'shard')
- hidden_second_new: float32 [2, 2048], P(None, 'shard')
- vector_second_new: float32 [53, 512], P(None, 'shard')
- row_update: float32 [512, 8192], P('shard')
- down_update: float32 [2, 2048, 512], P(None, 'shard')
- hidden_update: float32 [2, 2048], P(None, 'shard')
- vector_update: float32 [53, 512], P(None, 'shard')
The draws below stay inside these ranges and needn't reach their ends.
All inputs are finite; a program needn't handle non-finite values.
Results may differ from the reference program's by a relative error of at most 0.018.
Values may be sent and summed in bfloat16 or wider, within the bound.
No kernel may reach another device: no remote copies, remote signals or barrier semaphores. Data moves between devices by JAX's collectives and lax.ppermute only.
A program may use at most 384 MiB of HBM per device.

```python
import math
import jax
import jax.numpy as jnp
from jax import lax

D = 512
HEADS = 8
HEAD = 64
FF = 2048
KERNEL = 31
CLIP_LEN = 750
CLIPS = 64
TOKENS = 48000
MCOLS = 8192
NVEC = 53


def clip_levels():
    return 0.5 + jnp.arange(CLIPS).astype(jnp.float32) / max(CLIPS - 1, 1)


def draw_inputs(key, part):
    noise_key = jax.random.fold_in(key, 21)
    common_key = jax.random.fold_in(key, 22)
    pattern_key = jax.random.fold_in(key, 23)
    clip_level = clip_levels()
    common = jnp.clip(jax.random.normal(common_key, (D,), jnp.float32), -3.0, 3.0)
    pattern = jnp.clip(jax.random.normal(pattern_key, (CLIPS, D), jnp.float32), -3.0, 3.0)
    offset = clip_level[:, None, None] * (0.6 * common[None, :] + pattern)[:, None, :]
    noise_part = jnp.clip(jax.random.normal(noise_key, (CLIPS, CLIP_LEN, D), jnp.float32), -4.0, 4.0)
    return (noise_part + offset).astype(jnp.bfloat16)


def draw_cotangent(key, part):
    noise_key = jax.random.fold_in(key, 31)
    clip_level = clip_levels()
    noise_part = jnp.clip(jax.random.normal(noise_key, (CLIPS, CLIP_LEN, D), jnp.float32), -4.0, 4.0)
    return noise_part * clip_level[:, None, None]


def draw_row_weights(key, part):
    width = 2 * FF + 8 * D
    base_values = jnp.clip(jax.random.normal(key, (D, width), jnp.float32), -4.0, 4.0)
    column = jnp.arange(width)
    begin_col = 2 * FF + 6 * D
    boost = jnp.where((column >= begin_col) & (column < begin_col + D), 8.0, 1.0)
    return (base_values * boost[None, :] * D ** (-0.5)).astype(jnp.bfloat16)


def draw_vectors(key, part):
    row_total = 22 + KERNEL
    gain_key = jax.random.fold_in(key, 41)
    bias_key = jax.random.fold_in(key, 42)
    tap_key = jax.random.fold_in(key, 43)
    index = jnp.arange(row_total)[:, None]
    is_gain = (index == 0) | (index == 3) | (index == 10) | (index == 15) | (index == 17) | (index == 20)
    is_kernel = index >= 22
    gain_entries = jax.random.uniform(gain_key, (row_total, D), jnp.float32, minval=0.5, maxval=1.5)
    bias_values = jax.random.uniform(bias_key, (row_total, D), jnp.float32, minval=-0.5, maxval=0.5)
    tap_values = jnp.clip(jax.random.normal(tap_key, (row_total, D), jnp.float32), -3.0, 3.0) * KERNEL ** (-0.5)
    return jnp.where(is_gain, gain_entries, jnp.where(is_kernel, tap_values, bias_values)).astype(jnp.bfloat16)


def levels(key, dims, cuts, least, high):
    def one(dim, shards_of):
        heights = jax.random.uniform(jax.random.fold_in(jax.random.fold_in(key, 6), dim), (shards_of,), jnp.float32, least / len(cuts), high / len(cuts))
        return jnp.repeat(jnp.exp(heights), dims[dim] // shards_of).reshape((-1,) + (1,) * (len(dims) - dim - 1))

    loudness = one(*cuts[0])
    for cut in cuts[1:]:
        loudness = loudness * one(*cut)
    return loudness


def normal_values(stream_key, dims, scale, reach, cuts=(), kind=jnp.bfloat16):
    gain = levels(stream_key, dims, cuts, -0.22, 0.18) if cuts else 1.0
    entries = jax.random.normal(stream_key, dims, jnp.float32) * scale * gain
    return jnp.minimum(jnp.maximum(entries, -reach), reach).astype(kind)


def setup_inputs(seed: int = 0) -> dict:
    arg_keys = jax.random.split(jax.random.key(seed), 16)
    inputs = draw_inputs(jax.random.fold_in(arg_keys[15], 71), 0)
    cotangent = draw_cotangent(jax.random.fold_in(arg_keys[15], 71), 0)
    row_weights = draw_row_weights(jax.random.fold_in(arg_keys[15], 71), 0)
    down_weights = normal_values(arg_keys[3], (2, FF, D), FF ** -0.5, 0.125, ((1, 8),))
    hidden_bias = jnp.clip(jax.random.uniform(arg_keys[4], (2, FF), jnp.float32, -0.5, 0.5) * levels(arg_keys[4], (2, FF), ((1, 8),), -0.4, 0.0), -0.5, 0.5).astype(jnp.bfloat16)
    vectors = draw_vectors(jax.random.fold_in(arg_keys[15], 71), 0)
    row_first = normal_values(arg_keys[6], (D, MCOLS), (0.05 * TOKENS ** 0.5), 64.0, ((0, 8),), jnp.float32)
    down_first = normal_values(arg_keys[7], (2, FF, D), (0.05 * TOKENS ** 0.5), 64.0, ((1, 8),), jnp.float32)
    hidden_first = normal_values(arg_keys[8], (2, FF), (0.05 * TOKENS ** 0.5), 64.0, ((1, 8),), jnp.float32)
    vector_first = normal_values(arg_keys[9], (NVEC, D), (0.05 * TOKENS ** 0.5), 64.0, ((1, 8),), jnp.float32)
    row_second = jnp.clip(24.0 + 216.0 * jax.random.uniform(arg_keys[10], (D, MCOLS), jnp.float32) ** levels(arg_keys[10], (D, MCOLS), ((0, 8),), -0.2, 0.2), 24.0, 240.0)
    down_second = jnp.clip(24.0 + 216.0 * jax.random.uniform(arg_keys[11], (2, FF, D), jnp.float32) ** levels(arg_keys[11], (2, FF, D), ((1, 8),), -0.2, 0.2), 24.0, 240.0)
    hidden_second = jnp.clip(24.0 + 216.0 * jax.random.uniform(arg_keys[12], (2, FF), jnp.float32) ** levels(arg_keys[12], (2, FF), ((1, 8),), -0.2, 0.2), 24.0, 240.0)
    vector_second = jnp.clip(24.0 + 216.0 * jax.random.uniform(arg_keys[13], (NVEC, D), jnp.float32) ** levels(arg_keys[13], (NVEC, D), ((1, 8),), -0.2, 0.2), 24.0, 240.0)
    step_number = jax.random.randint(arg_keys[14], (1,), 1, 21).astype(jnp.int32)
    return dict(inputs=inputs, cotangent=cotangent, row_weights=row_weights, down_weights=down_weights, hidden_bias=hidden_bias, vectors=vectors, row_first=row_first, down_first=down_first, hidden_first=hidden_first, vector_first=vector_first, row_second=row_second, down_second=down_second, hidden_second=hidden_second, vector_second=vector_second, step_number=step_number)


@jax.custom_vjp
def low(v):
    return lax.optimization_barrier(v.astype(jnp.bfloat16)).astype(jnp.float32)

@jax.custom_vjp
def low_back(v):
    return v

def low_keep(v):
    return (low(v), None)

def low_pass(kept, grad):
    return (grad,)

def back_keep(v):
    return (v, None)

def back_low(kept, grad):
    return (low(grad),)
low.defvjp(low_keep, low_pass)
low_back.defvjp(back_keep, back_low)
maximum_precision = lax.Precision.HIGHEST
norm_eps = 1e-05
beta_first = 0.9
beta_second = 0.99
learn_rate = 0.01
weight_decay = 0.1
adam_eps = 1e-08
front_gain = 0
front_shift = 1
front_out = 2
attend_gain = 3
attend_shift = 4
query_bias = 5
value_bias = 6
attend_out = 7
content_bias = 8
position_bias = 9
conv_gain = 10
conv_shift = 11
glu_value = 12
glu_gate = 13
conv_out = 14
batch_gain = 15
batch_shift = 16
back_gain = 17
back_shift = 18
back_out = 19
final_gain = 20
final_shift = 21
kernel_start = 22

def product(left, right):
    return jnp.dot(left, right, precision=maximum_precision, preferred_element_type=jnp.float32)

def swish_act(values):
    return values * jax.nn.sigmoid(values)

def layer_norm(residual, gain_vec, shift_vec):
    average = lax.optimization_barrier(jnp.mean(residual, axis=-1, keepdims=True))
    centered = residual - average
    spread = lax.optimization_barrier(jnp.mean(centered * centered, axis=-1, keepdims=True))
    return centered * lax.rsqrt(spread + norm_eps) * gain_vec + shift_vec

def position_table():
    offsets = (CLIP_LEN - 1 - jnp.arange(2 * CLIP_LEN - 1)).astype(jnp.float32)
    frequency = jnp.exp(jnp.arange(0, D, 2).astype(jnp.float32) * (-math.log(10000.0) / D))
    angles = offsets[:, None] * frequency[None, :]
    return jnp.stack([jnp.sin(angles), jnp.cos(angles)], axis=-1).reshape(2 * CLIP_LEN - 1, D)

def shift_rows(full_rows):
    leading = full_rows.shape[:-2]
    length = full_rows.shape[-2]
    padded = jnp.concatenate([jnp.zeros(leading + (length, 1), full_rows.dtype), full_rows], axis=-1)
    padded = padded.reshape(leading + (2 * length, length))[..., 1:, :]
    return padded.reshape(leading + (length, 2 * length - 1))[..., :length]

def depthwise(gated, kernel):
    margin = (KERNEL - 1) // 2
    padded = jnp.pad(gated, ((0, 0), (margin, margin), (0, 0)))
    summed = jnp.zeros_like(gated)
    for tap_index in range(KERNEL):
        summed = summed + kernel[tap_index] * padded[:, tap_index:tap_index + CLIP_LEN, :]
    return summed

def feed_forward(residual, w_in, bias_in, w_out, vectors, first_row):
    normed = low(layer_norm(residual, vectors[first_row], vectors[first_row + 1]))
    hidden = low_back(product(normed, w_in)) + bias_in
    active = low(swish_act(hidden))
    return residual + 0.5 * (low_back(product(active, w_out)) + vectors[first_row + 2])

def forward(inputs, row_weights, down_weights, hidden_bias, vectors):
    clip_count = inputs.shape[0]
    residual = inputs.reshape(clip_count * CLIP_LEN, D)
    offset_cols = 2 * FF
    w_query = row_weights[:, offset_cols:offset_cols + D]
    w_key = row_weights[:, offset_cols + D:offset_cols + 2 * D]
    w_value = row_weights[:, offset_cols + 2 * D:offset_cols + 3 * D]
    w_place = row_weights[:, offset_cols + 3 * D:offset_cols + 4 * D]
    w_glu = row_weights[:, offset_cols + 4 * D:offset_cols + 6 * D]
    w_attend = row_weights[:, offset_cols + 6 * D:offset_cols + 7 * D]
    w_point = row_weights[:, offset_cols + 7 * D:]
    front = feed_forward(residual, row_weights[:, :FF], hidden_bias[0], down_weights[0], vectors, front_gain)
    normed = low(layer_norm(front, vectors[attend_gain], vectors[attend_shift]))
    queries = low_back(product(normed, w_query)) + vectors[query_bias]
    query_content = low(queries + vectors[content_bias])
    query_position = low(queries + vectors[position_bias])
    key_rows = low(low_back(product(normed, w_key)))
    value_rows = low(low_back(product(normed, w_value)) + vectors[value_bias])
    table_low = low(position_table())
    scale_factor = 1.0 / math.sqrt(HEAD)

    def one_clip(pieces):
        single_head_width = [member.reshape(CLIP_LEN, HEADS, HEAD) for member in pieces]
        location_table_lines = low(low_back(product(table_low, w_place))).reshape(2 * CLIP_LEN - 1, HEADS, HEAD)
        content = jnp.einsum('ihd,jhd->hij', single_head_width[0], single_head_width[2], precision=maximum_precision)
        relative_shifted = jnp.einsum('kfs,bfs->fkb', single_head_width[1], location_table_lines, precision=maximum_precision)
        scores = low_back(content + shift_rows(relative_shifted)) * scale_factor
        largest = lax.optimization_barrier(jnp.max(scores, axis=-1, keepdims=True))
        exponent = jnp.exp(scores - largest)
        weights = exponent / lax.optimization_barrier(jnp.sum(exponent, axis=-1, keepdims=True))
        context = jnp.einsum('hij,jhd->ihd', low(weights), single_head_width[3], precision=maximum_precision)
        return low(low_back(context)).reshape(CLIP_LEN, D)
    stacked = tuple((member.reshape(clip_count, CLIP_LEN, D) for member in (query_content, query_position, key_rows, value_rows)))
    context = lax.map(jax.checkpoint(one_clip), stacked).reshape(clip_count * CLIP_LEN, D)
    attended = front + low_back(product(context, w_attend)) + vectors[attend_out]
    normed_conv = low(layer_norm(attended, vectors[conv_gain], vectors[conv_shift]))
    glu_pre = low_back(product(normed_conv, w_glu)) + jnp.concatenate([vectors[glu_value], vectors[glu_gate]])
    gated = glu_pre[:, :D] * jax.nn.sigmoid(glu_pre[:, D:])
    depth_out = depthwise(gated.reshape(clip_count, CLIP_LEN, D), vectors[kernel_start:kernel_start + KERNEL])
    mean_depth = lax.optimization_barrier(jnp.mean(depth_out, axis=(0, 1)))
    centered = depth_out - mean_depth
    var_depth = lax.optimization_barrier(jnp.mean(centered * centered, axis=(0, 1)))
    normed_batch = centered * lax.rsqrt(var_depth + norm_eps) * vectors[batch_gain] + vectors[batch_shift]
    active = low(swish_act(normed_batch)).reshape(clip_count * CLIP_LEN, D)
    convolved = attended + low_back(product(active, w_point)) + vectors[conv_out]
    back_field = feed_forward(convolved, row_weights[:, FF:offset_cols], hidden_bias[1], down_weights[1], vectors, back_gain)
    outputs = layer_norm(back_field, vectors[final_gain], vectors[final_shift])
    return outputs.reshape(clip_count, CLIP_LEN, D)

def adam_step(weight, gradient, first, second, count_steps):
    first_new = beta_first * first + (1.0 - beta_first) * gradient
    second_new = beta_second * second + (1.0 - beta_second) * gradient * gradient
    first_fix = 1.0 - jnp.power(beta_first, count_steps)
    second_fix = 1.0 - jnp.power(beta_second, count_steps)
    update = -learn_rate * (first_new / first_fix / (jnp.sqrt(second_new / second_fix) + adam_eps) + weight_decay * weight)
    return (first_new, second_new, update)

def reference(inputs, cotangent, row_weights, down_weights, hidden_bias, vectors, row_first, down_first, hidden_first, vector_first, row_second, down_second, hidden_second, vector_second, step_number):
    weights = (row_weights.astype(jnp.float32), down_weights.astype(jnp.float32), hidden_bias.astype(jnp.float32), vectors.astype(jnp.float32))
    outputs, pull_back = jax.vjp(forward, inputs.astype(jnp.float32), weights[0], weights[1], weights[2], weights[3])
    gradients = pull_back(cotangent.astype(jnp.float32))
    count_steps = step_number[0].astype(jnp.float32)
    row_new = adam_step(weights[0], gradients[1], row_first, row_second, count_steps)
    down_new = adam_step(weights[1], gradients[2], down_first, down_second, count_steps)
    latent_matrix_revised = adam_step(weights[2], gradients[3], hidden_first, hidden_second, count_steps)
    array_revised = adam_step(weights[3], gradients[4], vector_first, vector_second, count_steps)
    return (outputs, gradients[0], gradients[1], gradients[2], gradients[3], gradients[4], row_new[0], down_new[0], latent_matrix_revised[0], array_revised[0], row_new[1], down_new[1], latent_matrix_revised[1], array_revised[1], row_new[2], down_new[2], latent_matrix_revised[2], array_revised[2])
```

```python
import math

import jax
import jax.numpy as jnp
from jax import lax
from jax.experimental import pallas as pl
from jax.experimental.pallas import tpu as pltpu
from jax.sharding import PartitionSpec as P

D = 512
HEADS = 8
HEAD = 64
FF = 2048
KERNEL = 31
CLIP_LEN = 750
ROWS = 768
HALF = D // 2
PAIR = 2 * HEAD
PAIRS = HEADS // 2


norm_eps = 1e-05
beta_first = 0.9
beta_second = 0.99
learn_rate = 0.01
weight_decay = 0.1
adam_eps = 1e-08
front_gain = 0
attend_gain = 3
attend_shift = 4
query_bias = 5
value_bias = 6
attend_out = 7
content_bias = 8
position_bias = 9
conv_gain = 10
conv_shift = 11
glu_value = 12
glu_gate = 13
conv_out = 14
batch_gain = 15
batch_shift = 16
back_gain = 17
final_gain = 20
final_shift = 21
kernel_start = 22


def product(left, right):
    return jnp.dot(left, right, preferred_element_type=jnp.float32)


def left_factor(left, right):
    return lax.dot_general(
        left, right, (((0,), (0,)), ((), ())), preferred_element_type=jnp.float32
    )


def product_right(left, right):
    return lax.dot_general(
        left, right, (((1,), (1,)), ((), ())), preferred_element_type=jnp.float32
    )


def swish_act(values):
    return values * jax.nn.sigmoid(values)


def swish_slope(values):
    logistic = jax.nn.sigmoid(values)
    return logistic * (1.0 + values * (1.0 - logistic))


def norm_forward(residual, gain_vec, shift_vec):
    average = jnp.mean(residual, axis=-1, keepdims=True)
    centered = residual - average
    spread = jnp.mean(centered * centered, axis=-1, keepdims=True)
    inverse = lax.rsqrt(spread + norm_eps)
    unit_field = centered * inverse
    return (unit_field * gain_vec + shift_vec, unit_field, inverse)


def norm_backward(grad_out, unit_field, inverse, gain_vec):
    grad_unit = grad_out * gain_vec
    grad_field = inverse * (
        grad_unit
        - jnp.mean(grad_unit, axis=-1, keepdims=True)
        - unit_field * jnp.mean(grad_unit * unit_field, axis=-1, keepdims=True)
    )
    return (grad_field, jnp.sum(grad_out * unit_field, axis=0), jnp.sum(grad_out, axis=0))


def angle_tables():
    frequency = jnp.exp(jnp.arange(0, D, 2).astype(jnp.float32) * (-math.log(10000.0) / D))
    coarse = (32 * jnp.arange(ROWS // 32)).astype(jnp.float32)[:, None] * frequency
    fine = jnp.arange(32).astype(jnp.float32)[:, None] * frequency
    sin_c, cos_c = jnp.sin(coarse)[:, None], jnp.cos(coarse)[:, None]
    sin_f, cos_f = jnp.sin(fine)[None], jnp.cos(fine)[None]
    sine = (sin_c * cos_f + cos_c * sin_f).reshape(ROWS, HALF)
    cosine = (cos_c * cos_f - sin_c * sin_f).reshape(ROWS, HALF)
    stacked = (jnp.concatenate([cosine, sine], axis=1) * HEAD**-0.5).astype(jnp.bfloat16)
    return sine.T, cosine.T, stacked, stacked.T


def dot_nn(left, right):
    return lax.dot_general(
        left, right, (((1,), (0,)), ((), ())), preferred_element_type=jnp.float32
    )


def head_mask(values, head):
    lane = lax.broadcasted_iota(jnp.int32, values.shape, 1)
    inside = lane < HEAD if head == 0 else lane >= HEAD
    return jnp.where(inside, values, jnp.zeros_like(values))


def head_scores(query_content, query_position, keys_scaled, place, sine, cosine, stacked):
    lifted = product_right(place, query_position)
    lift_s, lift_c = lifted[:HALF], lifted[HALF:]
    turned = jnp.concatenate(
        [lift_s * sine + lift_c * cosine, lift_c * sine - lift_s * cosine], axis=0
    ).astype(jnp.bfloat16)
    return product_right(keys_scaled, query_content) + dot_nn(stacked, turned)


def key_valid():
    return lax.broadcasted_iota(jnp.int32, (ROWS, ROWS), 0) < CLIP_LEN


def attend_kernel(
    content_ref, position_ref, key_ref, value_ref, place_ref, sine_ref, cosine_ref, stacked_ref,
    context_ref, total_ref,
):
    query_content, query_position = content_ref[0], position_ref[0]
    keys = key_ref[0] * jnp.bfloat16(HEAD**-0.5)
    values = value_ref[0]
    place = place_ref[...]
    parts = []
    for head in range(2):
        scores = head_scores(
            query_content,
            query_position,
            head_mask(keys, head),
            head_mask(place, head),
            sine_ref[...],
            cosine_ref[...],
            stacked_ref[...],
        )
        scores = jnp.where(key_valid(), scores, -1e30)
        largest = jnp.max(scores, axis=0, keepdims=True)
        weights = jnp.exp(scores - largest)
        total = jnp.sum(weights, axis=0, keepdims=True)
        mixed = left_factor(values, weights.astype(jnp.bfloat16)) * (1.0 / total)
        parts.append(mixed[:HEAD] if head == 0 else mixed[HEAD:])
        total_ref[0, 0, head : head + 1, :] = largest + jnp.log(total)
    context_ref[0] = jnp.concatenate(parts, axis=0).T.astype(jnp.bfloat16)


def attend_back_kernel(
    content_ref, position_ref, key_ref, value_ref, grad_ref, total_ref, place_ref, sine_ref,
    cosine_ref, stacked_ref, stacked_t_ref,
    grad_query_ref, grad_key_ref, grad_value_ref, sums_ref, grad_place_ref,
):
    query_content, query_position = content_ref[0], position_ref[0]
    keys = key_ref[0] * jnp.bfloat16(HEAD**-0.5)
    values = value_ref[0]
    grad_context = grad_ref[0]
    place = place_ref[...]
    sine, cosine = sine_ref[...], cosine_ref[...]
    content_parts, position_parts = [], []
    grad_keys = grad_values = grad_place = None
    for head in range(2):
        keys_head, place_head = head_mask(keys, head), head_mask(place, head)
        scores = head_scores(
            query_content, query_position, keys_head, place_head, sine, cosine, stacked_ref[...]
        )
        weights = jnp.where(
            key_valid(), jnp.exp(scores - total_ref[0, 0, head : head + 1, :]), 0.0
        )
        grad_head = head_mask(grad_context, head)
        grad_weights = product_right(values, grad_head)
        value_part = dot_nn(weights.astype(jnp.bfloat16), grad_head)
        leaning = weights * grad_weights
        delta = jnp.sum(leaning, axis=0, keepdims=True)
        grad_scores = (leaning - weights * delta).astype(jnp.bfloat16)
        content_head = head_mask(query_content, head) * jnp.bfloat16(HEAD**-0.5)
        key_part = dot_nn(grad_scores, content_head)
        content_parts.append(left_factor(keys_head, grad_scores))
        turned = dot_nn(stacked_t_ref[...], grad_scores)
        turn_c, turn_s = turned[:HALF], turned[HALF:]
        lifted = jnp.concatenate(
            [turn_c * sine - turn_s * cosine, turn_c * cosine + turn_s * sine], axis=0
        ).astype(jnp.bfloat16)
        position_parts.append(left_factor(place_head, lifted))
        place_part = dot_nn(lifted, head_mask(query_position, head))
        if head == 0:
            grad_keys, grad_values, grad_place = key_part, value_part, place_part
        else:
            grad_keys += key_part
            grad_values += value_part
            grad_place += place_part
    grad_content = (content_parts[0] + content_parts[1]).T
    grad_position = (position_parts[0] + position_parts[1]).T
    grad_query_ref[0] = (grad_content + grad_position).astype(jnp.bfloat16)
    grad_key_ref[0] = grad_keys.astype(jnp.bfloat16)
    grad_value_ref[0] = grad_values.astype(jnp.bfloat16)
    sums_ref[0, 0] = jnp.concatenate(
        [
            jnp.sum(grad_content, axis=0, keepdims=True),
            jnp.sum(grad_position, axis=0, keepdims=True),
            jnp.sum(grad_values, axis=0, keepdims=True),
            jnp.zeros((5, PAIR), jnp.float32),
        ],
        axis=0,
    )

    @pl.when(pl.program_id(1) == 0)
    def _():
        grad_place_ref[...] = grad_place

    @pl.when(pl.program_id(1) != 0)
    def _():
        grad_place_ref[...] += grad_place


def clip_block(offset=0):
    return pl.BlockSpec((1, ROWS, PAIR), lambda pair, clip: (clip, 0, pair + offset))


def whole_block(shape):
    return pl.BlockSpec(shape, lambda pair, clip: (0,) * len(shape))


def pair_block(rows):
    return pl.BlockSpec((1, 1, rows, ROWS), lambda pair, clip: (clip, pair, 0, 0))


def attend_call(query_content, query_position, key_rows, value_rows, place, tables):
    clip_count = query_content.shape[0]
    sine, cosine, stacked, _ = tables
    return pl.pallas_call(
        attend_kernel,
        grid=(PAIRS, clip_count),
        in_specs=[clip_block()] * 4
        + [
            pl.BlockSpec((D, PAIR), lambda pair, clip: (0, pair)),
            whole_block((HALF, ROWS)),
            whole_block((HALF, ROWS)),
            whole_block((ROWS, D)),
        ],
        out_specs=[clip_block(), pair_block(2)],
        out_shape=[
            jax.ShapeDtypeStruct((clip_count, ROWS, D), jnp.bfloat16),
            jax.ShapeDtypeStruct((clip_count, PAIRS, 2, ROWS), jnp.float32),
        ],
        compiler_params=pltpu.CompilerParams(vmem_limit_bytes=56 << 20),
    )(query_content, query_position, key_rows, value_rows, place, sine, cosine, stacked)


def attend_back_call(
    query_content, query_position, key_rows, value_rows, grad_context, totals, place, tables
):
    clip_count = query_content.shape[0]
    sine, cosine, stacked, stacked_t = tables
    return pl.pallas_call(
        attend_back_kernel,
        grid=(PAIRS, clip_count),
        in_specs=[clip_block()] * 5
        + [
            pair_block(2),
            pl.BlockSpec((D, PAIR), lambda pair, clip: (0, pair)),
            whole_block((HALF, ROWS)),
            whole_block((HALF, ROWS)),
            whole_block((ROWS, D)),
            whole_block((D, ROWS)),
        ],
        out_specs=[clip_block()] * 3
        + [
            pl.BlockSpec((1, 1, 8, PAIR), lambda pair, clip: (clip, pair, 0, 0)),
            pl.BlockSpec((D, PAIR), lambda pair, clip: (0, pair)),
        ],
        out_shape=[jax.ShapeDtypeStruct((clip_count, ROWS, D), jnp.bfloat16)] * 3
        + [
            jax.ShapeDtypeStruct((clip_count, PAIRS, 8, PAIR), jnp.float32),
            jax.ShapeDtypeStruct((D, D), jnp.float32),
        ],
        compiler_params=pltpu.CompilerParams(vmem_limit_bytes=56 << 20),
    )(
        query_content, query_position, key_rows, value_rows, grad_context, totals, place,
        sine, cosine, stacked, stacked_t,
    )


def depthwise(gated, kernel):
    margin = (KERNEL - 1) // 2
    padded = jnp.pad(gated, ((0, 0), (margin, margin), (0, 0)))
    summed = jnp.zeros_like(gated)
    for tap_index in range(KERNEL):
        summed = summed + kernel[tap_index] * padded[:, tap_index : tap_index + ROWS, :]
    return summed


def depthwise_back(grad_out, gated, kernel):
    margin = (KERNEL - 1) // 2
    padded_grad = jnp.pad(grad_out, ((0, 0), (margin, margin), (0, 0)))
    padded_gated = jnp.pad(gated, ((0, 0), (margin, margin), (0, 0)))
    grad_gated = jnp.zeros_like(gated)
    kernel_rows = []
    for tap_index in range(KERNEL):
        begin_row = 2 * margin - tap_index
        grad_gated = (
            grad_gated + kernel[tap_index] * padded_grad[:, begin_row : begin_row + ROWS, :]
        )
        kernel_rows.append(
            jnp.sum(grad_out * padded_gated[:, tap_index : tap_index + ROWS, :], axis=(0, 1))
        )
    return (grad_gated, jnp.stack(kernel_rows))


def ffn_forward(residual, w_in, bias_in, w_out, vector_full, first_row):
    normed, unit_field, inverse = norm_forward(
        residual, vector_full[first_row], vector_full[first_row + 1]
    )
    normed = normed.astype(jnp.bfloat16)
    hidden = product(normed, w_in) + bias_in
    active = swish_act(hidden).astype(jnp.bfloat16)
    result = residual + 0.5 * (product(active, w_out) + vector_full[first_row + 2])
    return (result, (normed, unit_field, inverse, hidden, active))


def perceptron_reverse(grad_field, saved, w_in, w_out, vector_full, first_row):
    normed, unit_field, inverse, hidden, active = saved
    bisected_value = 0.5 * grad_field
    halved_low = bisected_value.astype(jnp.bfloat16)
    grad_out_weight = left_factor(active, halved_low)
    grad_active = product_right(halved_low, w_out)
    grad_hidden = grad_active * swish_slope(hidden)
    hidden_low = grad_hidden.astype(jnp.bfloat16)
    grad_in_weight = left_factor(normed, hidden_low)
    grad_normed = product_right(hidden_low, w_in)
    grad_input, grad_gain, grad_shift = norm_backward(
        grad_normed, unit_field, inverse, vector_full[first_row]
    )
    return (
        grad_field + grad_input,
        (
            grad_in_weight,
            jnp.sum(grad_hidden, axis=0),
            grad_out_weight,
            grad_gain,
            grad_shift,
            jnp.sum(bisected_value, axis=0),
        ),
    )


def valid_rows(clip_count):
    token = lax.broadcasted_iota(jnp.int32, (clip_count, ROWS, 1), 1)
    return token < CLIP_LEN


def attend_forward(residual, w_triple, w_place, w_attend, vector_full, tables):
    row_count = residual.shape[0]
    clip_count = row_count // ROWS
    normed, unit_field, inverse = norm_forward(
        residual, vector_full[attend_gain], vector_full[attend_shift]
    )
    normed = normed.astype(jnp.bfloat16)
    triple = product(normed, w_triple)
    queries = triple[:, :D] + vector_full[query_bias]
    query_content = (queries + vector_full[content_bias]).astype(jnp.bfloat16)
    query_position = (queries + vector_full[position_bias]).astype(jnp.bfloat16)
    key_rows = triple[:, D : 2 * D].astype(jnp.bfloat16)
    value_rows = (triple[:, 2 * D :] + vector_full[value_bias]).astype(jnp.bfloat16)
    place = jnp.concatenate([w_place[0::2], w_place[1::2]], axis=0)
    packed = tuple(
        (
            member.reshape(clip_count, ROWS, D)
            for member in (query_content, query_position, key_rows, value_rows)
        )
    )
    context, totals = attend_call(*packed, place, tables)
    context = context.reshape(row_count, D)
    result = residual + product(context, w_attend) + vector_full[attend_out]
    return (result, (normed, unit_field, inverse, packed, place, context, totals))


def attend_backward(grad_field, saved, w_triple, w_attend, vector_full, tables):
    normed, unit_field, inverse, packed, place, context, totals = saved
    row_count = grad_field.shape[0]
    clip_count = row_count // ROWS
    grad_low = grad_field.astype(jnp.bfloat16)
    grad_attend = left_factor(context, grad_low)
    grad_context = (
        product_right(grad_low, w_attend).astype(jnp.bfloat16).reshape(clip_count, ROWS, D)
    )
    grad_queries, grad_keys, grad_values, sums, grad_place = attend_back_call(
        *packed, grad_context, totals, place, tables
    )
    grad_place_weight = jnp.stack([grad_place[:HALF], grad_place[HALF:]], axis=1).reshape(D, D)
    grad_triple = jnp.concatenate(
        [member.reshape(row_count, D) for member in (grad_queries, grad_keys, grad_values)],
        axis=1,
    )
    grad_triple_weight = left_factor(normed, grad_triple)
    grad_normed = product_right(grad_triple, w_triple)
    grad_input, grad_gain, grad_shift = norm_backward(
        grad_normed, unit_field, inverse, vector_full[attend_gain]
    )
    sums = jnp.sum(sums, axis=0).transpose(1, 0, 2).reshape(8, D)
    vector_rows = (
        grad_gain,
        grad_shift,
        sums[0] + sums[1],
        sums[2],
        jnp.sum(grad_field, axis=0),
        sums[0],
        sums[1],
    )
    return (
        grad_field + grad_input,
        grad_triple_weight,
        grad_place_weight,
        grad_attend,
        vector_rows,
    )


def conv_forward(residual, w_glu, w_point, vector_full):
    row_count = residual.shape[0]
    clip_count = row_count // ROWS
    normed, unit_field, inverse = norm_forward(
        residual, vector_full[conv_gain], vector_full[conv_shift]
    )
    normed = normed.astype(jnp.bfloat16)
    glu_pre = product(normed, w_glu) + jnp.concatenate(
        [vector_full[glu_value], vector_full[glu_gate]]
    )
    value_half = glu_pre[:, :D]
    gate_logistic = jax.nn.sigmoid(glu_pre[:, D:])
    valid = valid_rows(clip_count)
    gated = jnp.where(valid, (value_half * gate_logistic).reshape(clip_count, ROWS, D), 0.0)
    kernel = vector_full[kernel_start : kernel_start + KERNEL]
    depth_out = depthwise(gated, kernel)
    local_count = float(clip_count * CLIP_LEN)
    device_count = lax.axis_size("rep") * lax.axis_size("shard")
    token_count = device_count * local_count
    local_mean = jnp.sum(jnp.where(valid, depth_out, 0.0), axis=(0, 1)) / local_count
    local_square = jnp.sum(
        jnp.where(valid, (depth_out - local_mean) ** 2, 0.0), axis=(0, 1)
    )
    both = lax.all_gather(jnp.stack([local_mean, local_square]), ("rep", "shard"))
    mean_depth = jnp.mean(both[:, 0], axis=0)
    between = jnp.sum((both[:, 0] - mean_depth) ** 2, axis=0) * local_count
    var_depth = (jnp.sum(both[:, 1], axis=0) + between) / token_count
    centered = depth_out - mean_depth
    inverse_batch = lax.rsqrt(var_depth + norm_eps)
    unit_batch = centered * inverse_batch
    normed_batch = unit_batch * vector_full[batch_gain] + vector_full[batch_shift]
    active = swish_act(normed_batch).astype(jnp.bfloat16).reshape(row_count, D)
    result = residual + product(active, w_point) + vector_full[conv_out]
    return (
        result,
        (
            normed,
            unit_field,
            inverse,
            value_half,
            gate_logistic,
            gated,
            unit_batch,
            inverse_batch,
            normed_batch,
            active,
            token_count,
        ),
    )


def conv_backward(grad_field, saved, w_glu, w_point, vector_full):
    (
        normed,
        unit_field,
        inverse,
        value_half,
        gate_logistic,
        gated,
        unit_batch,
        inverse_batch,
        normed_batch,
        active,
        token_count,
    ) = saved
    row_count = grad_field.shape[0]
    clip_count = row_count // ROWS
    grad_low = grad_field.astype(jnp.bfloat16)
    grad_point = left_factor(active, grad_low)
    grad_active = product_right(grad_low, w_point).reshape(clip_count, ROWS, D)
    grad_norm = grad_active * swish_slope(normed_batch)
    local_shift = jnp.sum(grad_norm, axis=(0, 1))
    local_gain = jnp.sum(grad_norm * unit_batch, axis=(0, 1))
    total_shift, overall_multiplier = lax.psum(
        jnp.stack([local_shift, local_gain]), ("rep", "shard")
    )
    valid = valid_rows(clip_count)
    grad_depth = (
        vector_full[batch_gain]
        * inverse_batch
        * (grad_norm - total_shift / token_count - unit_batch * (overall_multiplier / token_count))
    )
    grad_depth = jnp.where(valid, grad_depth, 0.0)
    kernel = vector_full[kernel_start : kernel_start + KERNEL]
    grad_gated, grad_kernel = depthwise_back(grad_depth, gated, kernel)
    grad_gated = jnp.where(valid, grad_gated, 0.0).reshape(row_count, D)
    grad_value = grad_gated * gate_logistic
    grad_gate = grad_gated * value_half * gate_logistic * (1.0 - gate_logistic)
    glu_low = jnp.concatenate([grad_value, grad_gate], axis=1).astype(jnp.bfloat16)
    grad_glu_weight = left_factor(normed, glu_low)
    grad_normed = product_right(glu_low, w_glu)
    grad_input, grad_gain, grad_shift = norm_backward(
        grad_normed, unit_field, inverse, vector_full[conv_gain]
    )
    return (
        grad_field + grad_input,
        (
            grad_glu_weight,
            grad_point,
            grad_gain,
            grad_shift,
            jnp.sum(grad_value, axis=0),
            jnp.sum(grad_gate, axis=0),
            jnp.sum(grad_field, axis=0),
            local_gain,
            local_shift,
            grad_kernel,
        ),
    )


def adam_step(weight, gradient, first, second, count_steps):
    first_new = beta_first * first + (1.0 - beta_first) * gradient
    second_new = beta_second * second + (1.0 - beta_second) * gradient * gradient
    first_fix = 1.0 - jnp.power(beta_first, count_steps)
    second_fix = 1.0 - jnp.power(beta_second, count_steps)
    update = -learn_rate * (
        first_new / first_fix / (jnp.sqrt(second_new / second_fix) + adam_eps)
        + weight_decay * weight
    )
    return (first_new, second_new, update)


def shards(
    inputs,
    cotangent,
    row_weights,
    down_weights,
    hidden_bias,
    vectors,
    row_first,
    down_first,
    hidden_first,
    vector_first,
    row_second,
    down_second,
    hidden_second,
    vector_second,
    step_number,
):
    clip_count = inputs.shape[0]
    row_count = clip_count * ROWS
    shard_count = lax.axis_size("shard")
    offset_cols = 2 * FF
    hidden_cols = FF // shard_count
    vector_cols = D // shard_count
    hidden_lines = 2 * hidden_cols // vector_cols
    row_total = vectors.shape[0]

    def gather(piece):
        return lax.all_gather(piece, "shard", axis=0, tiled=True)

    small = lax.all_gather(
        jnp.concatenate([vectors, hidden_bias.reshape(hidden_lines, vector_cols)], axis=0), "shard"
    ).astype(jnp.float32)
    vector_full = small[:, :row_total].transpose(1, 0, 2).reshape(row_total, D)
    hidden_full = (
        small[:, row_total:].reshape(shard_count, 2, hidden_cols).transpose(1, 0, 2).reshape(2, FF)
    )
    w_front = gather(row_weights[:, :FF])
    down_front = gather(down_weights[0])
    w_rest = gather(row_weights[:, offset_cols:])
    w_back = gather(row_weights[:, FF:offset_cols])
    down_back = gather(down_weights[1])
    w_triple = w_rest[:, : 3 * D]
    w_place = w_rest[:, 3 * D : 4 * D]
    w_glu = w_rest[:, 4 * D : 6 * D]
    w_attend = w_rest[:, 6 * D : 7 * D]
    w_point = w_rest[:, 7 * D :]
    tables = angle_tables()
    extra = ((0, 0), (0, ROWS - CLIP_LEN), (0, 0))
    residual = jnp.pad(inputs, extra).reshape(row_count, D).astype(jnp.float32)
    cotangent_rows = jnp.pad(cotangent, extra).reshape(row_count, D)
    front, stored_leading_block = ffn_forward(
        residual, w_front, hidden_full[0], down_front, vector_full, front_gain
    )
    attended, saved_attend = attend_forward(
        front, w_triple, w_place, w_attend, vector_full, tables
    )
    convolved, saved_conv = conv_forward(attended, w_glu, w_point, vector_full)
    back_field, saved_back = ffn_forward(
        convolved, w_back, hidden_full[1], down_back, vector_full, back_gain
    )
    outputs, unit_final, inverse_final = norm_forward(
        back_field, vector_full[final_gain], vector_full[final_shift]
    )
    grad_back, final_gain_grad, final_shift_grad = norm_backward(
        cotangent_rows, unit_final, inverse_final, vector_full[final_gain]
    )
    grad_conv, back_grads = perceptron_reverse(
        grad_back, saved_back, w_back, down_back, vector_full, back_gain
    )
    grad_attended, conv_grads = conv_backward(grad_conv, saved_conv, w_glu, w_point, vector_full)
    grad_front, triple_grad, place_grad, attend_grad, attend_rows = attend_backward(
        grad_attended, saved_attend, w_triple, w_attend, vector_full, tables
    )
    grad_input, front_grads = perceptron_reverse(
        grad_front, stored_leading_block, w_front, down_front, vector_full, front_gain
    )
    hidden_grad = jnp.stack([front_grads[1], back_grads[1]])
    vector_rows = (
        [front_grads[3], front_grads[4], front_grads[5]]
        + list(attend_rows)
        + list(conv_grads[2:9])
        + [back_grads[3], back_grads[4], back_grads[5], final_gain_grad, final_shift_grad]
    )
    vector_grad = jnp.concatenate([jnp.stack(vector_rows), conv_grads[9]], axis=0)

    def reduce(piece):
        piece = lax.psum_scatter(
            piece.astype(jnp.bfloat16), "shard", scatter_dimension=0, tiled=True
        )
        return lax.psum(piece, "rep").astype(jnp.float32)

    back_sum = reduce(back_grads[0])
    down_back_sum = reduce(back_grads[2])
    conv_sum = reduce(jnp.concatenate([conv_grads[0], attend_grad, conv_grads[1]], axis=1))
    attend_sum = reduce(jnp.concatenate([triple_grad, place_grad], axis=1))
    down_front_sum = reduce(front_grads[2])
    front_sum = reduce(front_grads[0])
    small_grad = jnp.concatenate(
        [
            vector_grad.reshape(row_total, shard_count, vector_cols).transpose(1, 0, 2),
            hidden_grad.reshape(2, shard_count, hidden_cols)
            .transpose(1, 0, 2)
            .reshape(shard_count, hidden_lines, vector_cols),
        ],
        axis=1,
    )
    small_sum = lax.psum(small_grad, ("rep", "shard"))[lax.axis_index("shard")]
    owned_grads = (
        jnp.concatenate([front_sum, back_sum, attend_sum, conv_sum], axis=1),
        jnp.stack([down_front_sum, down_back_sum]),
        small_sum[row_total:].reshape(2, hidden_cols),
        small_sum[:row_total],
    )
    count_steps = step_number[0].astype(jnp.float32)
    row_new = adam_step(
        row_weights.astype(jnp.float32), owned_grads[0], row_first, row_second, count_steps
    )
    down_new = adam_step(
        down_weights.astype(jnp.float32), owned_grads[1], down_first, down_second, count_steps
    )
    latent_matrix_revised = adam_step(
        hidden_bias.astype(jnp.float32), owned_grads[2], hidden_first, hidden_second, count_steps
    )
    array_revised = adam_step(
        vectors.astype(jnp.float32), owned_grads[3], vector_first, vector_second, count_steps
    )
    return (
        outputs.reshape(clip_count, ROWS, D)[:, :CLIP_LEN],
        grad_input.reshape(clip_count, ROWS, D)[:, :CLIP_LEN],
        owned_grads[0],
        owned_grads[1],
        owned_grads[2],
        owned_grads[3],
        row_new[0],
        down_new[0],
        latent_matrix_revised[0],
        array_revised[0],
        row_new[1],
        down_new[1],
        latent_matrix_revised[1],
        array_revised[1],
        row_new[2],
        down_new[2],
        latent_matrix_revised[2],
        array_revised[2],
    )


def solution(mesh):
    in_specs = (
        P(("rep", "shard"), None, None),
        P(("rep", "shard"), None, None),
        P("shard", None),
        P(None, "shard", None),
        P(None, "shard"),
        P(None, "shard"),
        P("shard", None),
        P(None, "shard", None),
        P(None, "shard"),
        P(None, "shard"),
        P("shard", None),
        P(None, "shard", None),
        P(None, "shard"),
        P(None, "shard"),
        P(),
    )
    out_specs = (
        P(("rep", "shard"), None, None),
        P(("rep", "shard"), None, None),
        P("shard", None),
        P(None, "shard", None),
        P(None, "shard"),
        P(None, "shard"),
        P("shard", None),
        P(None, "shard", None),
        P(None, "shard"),
        P(None, "shard"),
        P("shard", None),
        P(None, "shard", None),
        P(None, "shard"),
        P(None, "shard"),
        P("shard", None),
        P(None, "shard", None),
        P(None, "shard"),
        P(None, "shard"),
    )
    return jax.shard_map(shards, mesh=mesh, in_specs=in_specs, out_specs=out_specs, check_vma=False)
```

```python
import math

import jax
import jax.numpy as jnp
from jax import lax
from jax.experimental import pallas as pl
from jax.experimental.pallas import tpu as pltpu
from jax.sharding import PartitionSpec as P

D = 512
HEADS = 8
HEAD = 64
FF = 2048
KERNEL = 31
CLIP_LEN = 750
ROWS = 768
HALF = D // 2
PAIR = 2 * HEAD
PAIRS = HEADS // 2
LANES = 128
MARGIN = 16


norm_eps = 1e-05
beta_first = 0.9
beta_second = 0.99
learn_rate = 0.01
weight_decay = 0.1
adam_eps = 1e-08
front_gain = 0
attend_gain = 3
attend_shift = 4
query_bias = 5
value_bias = 6
attend_out = 7
content_bias = 8
position_bias = 9
conv_gain = 10
conv_shift = 11
glu_value = 12
glu_gate = 13
conv_out = 14
batch_gain = 15
batch_shift = 16
back_gain = 17
final_gain = 20
final_shift = 21
kernel_start = 22


class Lines:
    def __init__(self, whole):
        self.whole = whole

    def __getitem__(self, line):
        return self.whole[line : line + 1]


def product(left, right):
    return jnp.dot(left, right, preferred_element_type=jnp.float32)


def left_factor(left, right):
    return lax.dot_general(
        left, right, (((0,), (0,)), ((), ())), preferred_element_type=jnp.float32
    )


def product_right(left, right):
    return lax.dot_general(
        left, right, (((1,), (1,)), ((), ())), preferred_element_type=jnp.float32
    )


def swish_act(values):
    return values * jax.nn.sigmoid(values)


def swish_slope(values):
    logistic = jax.nn.sigmoid(values)
    return logistic * (1.0 + values * (1.0 - logistic))


def norm_forward(residual, gain_vec, shift_vec):
    average = jnp.mean(residual, axis=-1, keepdims=True)
    centered = residual - average
    spread = jnp.mean(centered * centered, axis=-1, keepdims=True)
    inverse = lax.rsqrt(spread + norm_eps)
    unit_field = centered * inverse
    return (unit_field * gain_vec + shift_vec, unit_field, inverse)


def norm_backward(grad_out, unit_field, inverse, gain_vec):
    grad_unit = grad_out * gain_vec
    grad_field = inverse * (
        grad_unit
        - jnp.mean(grad_unit, axis=-1, keepdims=True)
        - unit_field * jnp.mean(grad_unit * unit_field, axis=-1, keepdims=True)
    )
    return (grad_field, jnp.sum(grad_out * unit_field, axis=0), jnp.sum(grad_out, axis=0))


def angle_tables():
    frequency = jnp.exp(jnp.arange(0, D, 2).astype(jnp.float32) * (-math.log(10000.0) / D))
    coarse = (32 * jnp.arange(ROWS // 32)).astype(jnp.float32)[:, None] * frequency
    fine = jnp.arange(32).astype(jnp.float32)[:, None] * frequency
    sin_c, cos_c = jnp.sin(coarse)[:, None], jnp.cos(coarse)[:, None]
    sin_f, cos_f = jnp.sin(fine)[None], jnp.cos(fine)[None]
    sine = (sin_c * cos_f + cos_c * sin_f).reshape(ROWS, HALF)
    cosine = (cos_c * cos_f - sin_c * sin_f).reshape(ROWS, HALF)
    stacked = (jnp.concatenate([cosine, sine], axis=1) * HEAD**-0.5).astype(jnp.bfloat16)
    return sine.T, cosine.T, stacked, stacked.T


def dot_nn(left, right):
    return lax.dot_general(
        left, right, (((1,), (0,)), ((), ())), preferred_element_type=jnp.float32
    )


def head_mask(values, head):
    lane = lax.broadcasted_iota(jnp.int32, values.shape, 1)
    inside = lane < HEAD if head == 0 else lane >= HEAD
    return jnp.where(inside, values, jnp.zeros_like(values))


def head_scores(query_content, query_position, keys_scaled, place, sine, cosine, stacked):
    lifted = product_right(place, query_position)
    lift_s, lift_c = lifted[:HALF], lifted[HALF:]
    turned = jnp.concatenate(
        [lift_s * sine + lift_c * cosine, lift_c * sine - lift_s * cosine], axis=0
    ).astype(jnp.bfloat16)
    return product_right(keys_scaled, query_content) + dot_nn(stacked, turned)


def key_valid():
    return lax.broadcasted_iota(jnp.int32, (ROWS, ROWS), 0) < CLIP_LEN


def attend_kernel(
    content_ref, position_ref, key_ref, value_ref, place_ref, sine_ref, cosine_ref, stacked_ref,
    context_ref, total_ref,
):
    query_content, query_position = content_ref[0], position_ref[0]
    keys = key_ref[0] * jnp.bfloat16(HEAD**-0.5)
    values = value_ref[0]
    place = place_ref[...]
    parts = []
    for head in range(2):
        scores = head_scores(
            query_content,
            query_position,
            head_mask(keys, head),
            head_mask(place, head),
            sine_ref[...],
            cosine_ref[...],
            stacked_ref[...],
        )
        scores = jnp.where(key_valid(), scores, -1e30)
        largest = jnp.max(scores, axis=0, keepdims=True)
        weights = jnp.exp(scores - largest)
        total = jnp.sum(weights, axis=0, keepdims=True)
        mixed = left_factor(values, weights.astype(jnp.bfloat16)) * (1.0 / total)
        parts.append(mixed[:HEAD] if head == 0 else mixed[HEAD:])
        total_ref[0, 0, head : head + 1, :] = largest + jnp.log(total)
    context_ref[0] = jnp.concatenate(parts, axis=0).T.astype(jnp.bfloat16)


def attend_back_kernel(
    content_ref, position_ref, key_ref, value_ref, grad_ref, total_ref, place_ref, sine_ref,
    cosine_ref, stacked_ref, stacked_t_ref,
    grad_query_ref, grad_key_ref, grad_value_ref, sums_ref, grad_place_ref,
):
    query_content, query_position = content_ref[0], position_ref[0]
    keys = key_ref[0] * jnp.bfloat16(HEAD**-0.5)
    values = value_ref[0]
    grad_context = grad_ref[0]
    place = place_ref[...]
    sine, cosine = sine_ref[...], cosine_ref[...]
    content_parts, position_parts = [], []
    grad_keys = grad_values = grad_place = None
    for head in range(2):
        keys_head, place_head = head_mask(keys, head), head_mask(place, head)
        scores = head_scores(
            query_content, query_position, keys_head, place_head, sine, cosine, stacked_ref[...]
        )
        weights = jnp.where(
            key_valid(), jnp.exp(scores - total_ref[0, 0, head : head + 1, :]), 0.0
        )
        grad_head = head_mask(grad_context, head)
        grad_weights = product_right(values, grad_head)
        value_part = dot_nn(weights.astype(jnp.bfloat16), grad_head)
        leaning = weights * grad_weights
        delta = jnp.sum(leaning, axis=0, keepdims=True)
        grad_scores = (leaning - weights * delta).astype(jnp.bfloat16)
        content_head = head_mask(query_content, head) * jnp.bfloat16(HEAD**-0.5)
        key_part = dot_nn(grad_scores, content_head)
        content_parts.append(left_factor(keys_head, grad_scores))
        turned = dot_nn(stacked_t_ref[...], grad_scores)
        turn_c, turn_s = turned[:HALF], turned[HALF:]
        lifted = jnp.concatenate(
            [turn_c * sine - turn_s * cosine, turn_c * cosine + turn_s * sine], axis=0
        ).astype(jnp.bfloat16)
        position_parts.append(left_factor(place_head, lifted))
        place_part = dot_nn(lifted, head_mask(query_position, head))
        if head == 0:
            grad_keys, grad_values, grad_place = key_part, value_part, place_part
        else:
            grad_keys += key_part
            grad_values += value_part
            grad_place += place_part
    grad_content = (content_parts[0] + content_parts[1]).T
    grad_position = (position_parts[0] + position_parts[1]).T
    grad_query_ref[0] = (grad_content + grad_position).astype(jnp.bfloat16)
    grad_key_ref[0] = grad_keys.astype(jnp.bfloat16)
    grad_value_ref[0] = grad_values.astype(jnp.bfloat16)
    sums_ref[0, 0] = jnp.concatenate(
        [
            jnp.sum(grad_content, axis=0, keepdims=True),
            jnp.sum(grad_position, axis=0, keepdims=True),
            jnp.sum(grad_values, axis=0, keepdims=True),
            jnp.zeros((5, PAIR), jnp.float32),
        ],
        axis=0,
    )

    @pl.when(pl.program_id(1) == 0)
    def _():
        grad_place_ref[...] = grad_place

    @pl.when(pl.program_id(1) != 0)
    def _():
        grad_place_ref[...] += grad_place


def clip_block(offset=0):
    return pl.BlockSpec((1, ROWS, PAIR), lambda pair, clip: (clip, 0, pair + offset))


def whole_block(shape):
    return pl.BlockSpec(shape, lambda pair, clip: (0,) * len(shape))


def pair_block(rows):
    return pl.BlockSpec((1, 1, rows, ROWS), lambda pair, clip: (clip, pair, 0, 0))


def attend_call(query_content, query_position, key_rows, value_rows, place, tables):
    clip_count = query_content.shape[0]
    sine, cosine, stacked, _ = tables
    return pl.pallas_call(
        attend_kernel,
        grid=(PAIRS, clip_count),
        in_specs=[clip_block()] * 4
        + [
            pl.BlockSpec((D, PAIR), lambda pair, clip: (0, pair)),
            whole_block((HALF, ROWS)),
            whole_block((HALF, ROWS)),
            whole_block((ROWS, D)),
        ],
        out_specs=[clip_block(), pair_block(2)],
        out_shape=[
            jax.ShapeDtypeStruct((clip_count, ROWS, D), jnp.bfloat16),
            jax.ShapeDtypeStruct((clip_count, PAIRS, 2, ROWS), jnp.float32),
        ],
        compiler_params=pltpu.CompilerParams(vmem_limit_bytes=56 << 20),
    )(query_content, query_position, key_rows, value_rows, place, sine, cosine, stacked)


def attend_back_call(
    query_content, query_position, key_rows, value_rows, grad_context, totals, place, tables
):
    clip_count = query_content.shape[0]
    sine, cosine, stacked, stacked_t = tables
    return pl.pallas_call(
        attend_back_kernel,
        grid=(PAIRS, clip_count),
        in_specs=[clip_block()] * 5
        + [
            pair_block(2),
            pl.BlockSpec((D, PAIR), lambda pair, clip: (0, pair)),
            whole_block((HALF, ROWS)),
            whole_block((HALF, ROWS)),
            whole_block((ROWS, D)),
            whole_block((D, ROWS)),
        ],
        out_specs=[clip_block()] * 3
        + [
            pl.BlockSpec((1, 1, 8, PAIR), lambda pair, clip: (clip, pair, 0, 0)),
            pl.BlockSpec((D, PAIR), lambda pair, clip: (0, pair)),
        ],
        out_shape=[jax.ShapeDtypeStruct((clip_count, ROWS, D), jnp.bfloat16)] * 3
        + [
            jax.ShapeDtypeStruct((clip_count, PAIRS, 8, PAIR), jnp.float32),
            jax.ShapeDtypeStruct((D, D), jnp.float32),
        ],
        compiler_params=pltpu.CompilerParams(vmem_limit_bytes=56 << 20),
    )(
        query_content, query_position, key_rows, value_rows, grad_context, totals, place,
        sine, cosine, stacked, stacked_t,
    )


def fill_margins(buffer, field):
    buffer[0:MARGIN, :] = jnp.zeros((MARGIN, LANES), jnp.float32)
    buffer[MARGIN : MARGIN + ROWS, :] = field
    buffer[MARGIN + ROWS :, :] = jnp.zeros((MARGIN, LANES), jnp.float32)


def slide(buffer, lines_ref, reverse, store):
    for begin in range(0, ROWS, LANES):
        summed = jnp.zeros((LANES, LANES), jnp.float32)
        for phase in range(8):
            span = buffer[begin + phase : begin + phase + LANES + 24, :]
            for block in range(4):
                tap = 8 * block + phase - 1
                if tap < 0:
                    continue
                line = kernel_start + (KERNEL - 1 - tap if reverse else tap)
                summed += lines_ref[line : line + 1, :] * span[8 * block : 8 * block + LANES]
        store(begin, summed)


def row_valid(begin):
    return lax.broadcasted_iota(jnp.int32, (LANES, LANES), 0) + begin < CLIP_LEN


def depthwise_kernel(gated_ref, lines_ref, depth_ref, stats_ref, buffer):
    fill_margins(buffer, gated_ref[0])

    def store(begin, summed):
        if begin + LANES > CLIP_LEN:
            summed = jnp.where(row_valid(begin), summed, 0.0)
        depth_ref[0, begin : begin + LANES, :] = summed

    slide(buffer, lines_ref, False, store)
    depth = depth_ref[0]
    mean = jnp.sum(depth, axis=0, keepdims=True) / CLIP_LEN
    token = lax.broadcasted_iota(jnp.int32, depth.shape, 0)
    centered = jnp.where(token < CLIP_LEN, depth - mean, 0.0)
    square = jnp.sum(centered * centered, axis=0, keepdims=True)
    stats_ref[0] = jnp.concatenate([mean, square, jnp.zeros((6, LANES), jnp.float32)], axis=0)


def depthwise_back_kernel(grad_ref, gated_ref, lines_ref, out_ref, taps_ref, buffer):
    fill_margins(buffer, grad_ref[0])

    def store(begin, summed):
        if begin + LANES > CLIP_LEN:
            summed = jnp.where(row_valid(begin), summed, 0.0)
        out_ref[0, begin : begin + LANES, :] = summed

    slide(buffer, lines_ref, True, store)
    fill_margins(buffer, gated_ref[0])

    @pl.when(pl.program_id(1) == 0)
    def _():
        taps_ref[...] = jnp.zeros((KERNEL + 1, LANES), jnp.float32)

    for phase in range(8):
        totals = [jnp.zeros((8, LANES), jnp.float32)] * 4
        for begin in range(0, ROWS, LANES):
            span = buffer[begin + phase : begin + phase + LANES + 24, :]
            grad = grad_ref[0, begin : begin + LANES, :]
            for block in range(4):
                if 8 * block + phase == 0:
                    continue
                both = grad * span[8 * block : 8 * block + LANES]
                totals[block] += jnp.sum(both.reshape(LANES // 8, 8, LANES), axis=0)
        for block in range(4):
            tap = 8 * block + phase - 1
            if tap >= 0:
                taps_ref[tap : tap + 1, :] += jnp.sum(totals[block], axis=0, keepdims=True)


def lane_block(rows):
    return pl.BlockSpec((1, rows, LANES), lambda lane, clip: (clip, 0, lane))


def line_block(rows):
    return pl.BlockSpec((rows, LANES), lambda lane, clip: (0, lane))


def depthwise(gated, lines):
    clip_count = gated.shape[0]
    return pl.pallas_call(
        depthwise_kernel,
        grid=(D // LANES, clip_count),
        in_specs=[lane_block(ROWS), line_block(lines.shape[0])],
        out_specs=[lane_block(ROWS), lane_block(8)],
        out_shape=[
            jax.ShapeDtypeStruct((clip_count, ROWS, D), jnp.float32),
            jax.ShapeDtypeStruct((clip_count, 8, D), jnp.float32),
        ],
        scratch_shapes=[pltpu.VMEM((ROWS + 2 * MARGIN, LANES), jnp.float32)],
    )(gated, lines)


def depthwise_back(grad_out, gated, lines):
    clip_count = gated.shape[0]
    grad_gated, taps = pl.pallas_call(
        depthwise_back_kernel,
        grid=(D // LANES, clip_count),
        in_specs=[lane_block(ROWS), lane_block(ROWS), line_block(lines.shape[0])],
        out_specs=[lane_block(ROWS), line_block(KERNEL + 1)],
        out_shape=[
            jax.ShapeDtypeStruct((clip_count, ROWS, D), jnp.float32),
            jax.ShapeDtypeStruct((KERNEL + 1, D), jnp.float32),
        ],
        scratch_shapes=[pltpu.VMEM((ROWS + 2 * MARGIN, LANES), jnp.float32)],
    )(grad_out, gated, lines)
    return grad_gated, taps[:KERNEL]


def swap(piece, axis, bit):
    size = lax.axis_size(axis)
    return lax.ppermute(piece, axis, [(place, place ^ bit) for place in range(size)])


def bits(axis):
    bit = 1
    while bit < lax.axis_size(axis):
        yield bit
        bit *= 2


def is_high(axis, bit):
    return (lax.axis_index(axis) // bit) % 2 == 1


def sum_everywhere(piece):
    for axis in ("rep", "shard"):
        for bit in bits(axis):
            piece = piece + swap(piece, axis, bit)
    return piece


def moments_everywhere(mean, square, count):
    for axis in ("rep", "shard"):
        for bit in bits(axis):
            other = swap(jnp.concatenate([mean, square], axis=0), axis, bit)
            apart = mean - other[:1]
            square = square + other[1:] + apart * apart * (0.5 * count)
            mean = 0.5 * (mean + other[:1])
            count = 2.0 * count
    return mean, square, count


def keep_half(low, high, axis, bit):
    upper = is_high(axis, bit)
    sent = jnp.where(upper, low, high).astype(jnp.bfloat16)
    kept = jnp.where(upper, high, low)
    return kept + swap(sent, axis, bit).astype(jnp.float32)


def reduce_piece(piece):
    shard_count = lax.axis_size("shard")
    rows = piece.shape[0] // shard_count
    for bit in bits("rep"):
        half = piece.shape[1] // 2
        piece = keep_half(piece[:, :half], piece[:, half:], "rep", bit)
    cols = piece.shape[1]
    for bit in bits("shard"):
        left = piece.shape[0] // rows
        view = piece.reshape(left // 2, 2, rows, cols)
        piece = keep_half(view[:, 0], view[:, 1], "shard", bit).reshape(left // 2 * rows, cols)
    piece = piece.astype(jnp.bfloat16)
    for bit in reversed(list(bits("rep"))):
        other = swap(piece, "rep", bit)
        upper = is_high("rep", bit)
        piece = jnp.concatenate(
            [jnp.where(upper, other, piece), jnp.where(upper, piece, other)], axis=1
        )
    return piece.astype(jnp.float32)


def gather_piece(piece):
    rows, cols = piece.shape
    shape = (1, rows, cols)
    piece = piece.reshape(shape)
    for bit in reversed(list(bits("shard"))):
        other = swap(piece, "shard", bit)
        upper = is_high("shard", bit)
        piece = jnp.stack(
            [jnp.where(upper, other, piece), jnp.where(upper, piece, other)], axis=1
        ).reshape(-1, rows, cols)
    return piece.reshape(-1, cols)


def gather_quarter(piece):
    cols = piece.shape[1]
    for bit in bits("rep"):
        half = piece.shape[1] // 2
        piece = jnp.where(is_high("rep", bit), piece[:, half:], piece[:, :half])
    piece = gather_piece(piece)
    for bit in reversed(list(bits("rep"))):
        other = swap(piece, "rep", bit)
        upper = is_high("rep", bit)
        piece = jnp.concatenate(
            [jnp.where(upper, other, piece), jnp.where(upper, piece, other)], axis=1
        )
    return piece


def ffn_forward(residual, w_in, bias_in, w_out, vector_full, first_row):
    normed, unit_field, inverse = norm_forward(
        residual, vector_full[first_row], vector_full[first_row + 1]
    )
    normed = normed.astype(jnp.bfloat16)
    hidden = product(normed, w_in) + bias_in
    active = swish_act(hidden).astype(jnp.bfloat16)
    result = residual + 0.5 * (product(active, w_out) + vector_full[first_row + 2])
    return (result, (normed, unit_field, inverse, hidden, active))


def perceptron_reverse(grad_field, saved, w_in, w_out, vector_full, first_row):
    normed, unit_field, inverse, hidden, active = saved
    bisected_value = 0.5 * grad_field
    halved_low = bisected_value.astype(jnp.bfloat16)
    grad_out_weight = left_factor(active, halved_low)
    grad_active = product_right(halved_low, w_out)
    grad_hidden = grad_active * swish_slope(hidden)
    hidden_low = grad_hidden.astype(jnp.bfloat16)
    grad_in_weight = left_factor(normed, hidden_low)
    grad_normed = product_right(hidden_low, w_in)
    grad_input, grad_gain, grad_shift = norm_backward(
        grad_normed, unit_field, inverse, vector_full[first_row]
    )
    return (
        grad_field + grad_input,
        (
            grad_in_weight,
            jnp.sum(grad_hidden, axis=0),
            grad_out_weight,
            grad_gain,
            grad_shift,
            jnp.sum(bisected_value, axis=0),
        ),
    )


def valid_rows(clip_count):
    token = lax.broadcasted_iota(jnp.int32, (clip_count, ROWS, 1), 1)
    return token < CLIP_LEN


def attend_forward(residual, w_triple, w_place, w_attend, vector_full, tables):
    row_count = residual.shape[0]
    clip_count = row_count // ROWS
    normed, unit_field, inverse = norm_forward(
        residual, vector_full[attend_gain], vector_full[attend_shift]
    )
    normed = normed.astype(jnp.bfloat16)
    triple = product(normed, w_triple)
    queries = triple[:, :D] + vector_full[query_bias]
    query_content = (queries + vector_full[content_bias]).astype(jnp.bfloat16)
    query_position = (queries + vector_full[position_bias]).astype(jnp.bfloat16)
    key_rows = triple[:, D : 2 * D].astype(jnp.bfloat16)
    value_rows = (triple[:, 2 * D :] + vector_full[value_bias]).astype(jnp.bfloat16)
    place = jnp.concatenate([w_place[0::2], w_place[1::2]], axis=0)
    packed = tuple(
        (
            member.reshape(clip_count, ROWS, D)
            for member in (query_content, query_position, key_rows, value_rows)
        )
    )
    context, totals = attend_call(*packed, place, tables)
    context = context.reshape(row_count, D)
    result = residual + product(context, w_attend) + vector_full[attend_out]
    return (result, (normed, unit_field, inverse, packed, place, context, totals))


def attend_backward(grad_field, saved, w_triple, w_attend, vector_full, tables):
    normed, unit_field, inverse, packed, place, context, totals = saved
    row_count = grad_field.shape[0]
    clip_count = row_count // ROWS
    grad_low = grad_field.astype(jnp.bfloat16)
    grad_attend = left_factor(context, grad_low)
    grad_context = (
        product_right(grad_low, w_attend).astype(jnp.bfloat16).reshape(clip_count, ROWS, D)
    )
    grad_queries, grad_keys, grad_values, sums, grad_place = attend_back_call(
        *packed, grad_context, totals, place, tables
    )
    grad_place_weight = jnp.stack([grad_place[:HALF], grad_place[HALF:]], axis=1).reshape(D, D)
    grad_triple = jnp.concatenate(
        [member.reshape(row_count, D) for member in (grad_queries, grad_keys, grad_values)],
        axis=1,
    )
    grad_triple_weight = left_factor(normed, grad_triple)
    grad_normed = product_right(grad_triple, w_triple)
    grad_input, grad_gain, grad_shift = norm_backward(
        grad_normed, unit_field, inverse, vector_full[attend_gain]
    )
    sums = jnp.sum(sums, axis=0).transpose(1, 0, 2).reshape(8, D)
    vector_rows = (
        grad_gain,
        grad_shift,
        sums[0] + sums[1],
        sums[2],
        jnp.sum(grad_field, axis=0),
        sums[0],
        sums[1],
    )
    return (
        grad_field + grad_input,
        grad_triple_weight,
        grad_place_weight,
        grad_attend,
        vector_rows,
    )


def conv_forward(residual, w_glu, w_point, vector_full):
    row_count = residual.shape[0]
    clip_count = row_count // ROWS
    normed, unit_field, inverse = norm_forward(
        residual, vector_full[conv_gain], vector_full[conv_shift]
    )
    normed = normed.astype(jnp.bfloat16)
    glu_pre = product(normed, w_glu) + jnp.concatenate(
        [vector_full[glu_value], vector_full[glu_gate]], axis=1
    )
    value_half = glu_pre[:, :D]
    gate_logistic = jax.nn.sigmoid(glu_pre[:, D:])
    valid = valid_rows(clip_count)
    gated = jnp.where(valid, (value_half * gate_logistic).reshape(clip_count, ROWS, D), 0.0)
    depth_out, stats = depthwise(gated, vector_full.whole)
    clip_mean, clip_square = stats[:, 0], stats[:, 1]
    local_mean = jnp.mean(clip_mean, axis=0, keepdims=True)
    local_square = jnp.sum(
        clip_square + CLIP_LEN * (clip_mean - local_mean) ** 2, axis=0, keepdims=True
    )
    mean_depth, square_depth, token_count = moments_everywhere(
        local_mean, local_square, float(clip_count * CLIP_LEN)
    )
    var_depth = square_depth / token_count
    centered = depth_out - mean_depth
    inverse_batch = lax.rsqrt(var_depth + norm_eps)
    unit_batch = centered * inverse_batch
    normed_batch = unit_batch * vector_full[batch_gain] + vector_full[batch_shift]
    active = swish_act(normed_batch).astype(jnp.bfloat16).reshape(row_count, D)
    result = residual + product(active, w_point) + vector_full[conv_out]
    return (
        result,
        (
            normed,
            unit_field,
            inverse,
            value_half,
            gate_logistic,
            gated,
            unit_batch,
            inverse_batch,
            normed_batch,
            active,
            token_count,
        ),
    )


def conv_backward(grad_field, saved, w_glu, w_point, vector_full):
    (
        normed,
        unit_field,
        inverse,
        value_half,
        gate_logistic,
        gated,
        unit_batch,
        inverse_batch,
        normed_batch,
        active,
        token_count,
    ) = saved
    row_count = grad_field.shape[0]
    clip_count = row_count // ROWS
    grad_low = grad_field.astype(jnp.bfloat16)
    grad_point = left_factor(active, grad_low)
    grad_active = product_right(grad_low, w_point).reshape(clip_count, ROWS, D)
    grad_norm = grad_active * swish_slope(normed_batch)
    local_shift = jnp.sum(grad_norm, axis=(0, 1))
    local_gain = jnp.sum(grad_norm * unit_batch, axis=(0, 1))
    totals = sum_everywhere(jnp.stack([local_shift, local_gain]))
    total_shift, overall_multiplier = totals[:1], totals[1:]
    valid = valid_rows(clip_count)
    grad_depth = (
        vector_full[batch_gain]
        * inverse_batch
        * (grad_norm - total_shift / token_count - unit_batch * (overall_multiplier / token_count))
    )
    grad_depth = jnp.where(valid, grad_depth, 0.0)
    grad_gated, grad_kernel = depthwise_back(grad_depth, gated, vector_full.whole)
    grad_gated = grad_gated.reshape(row_count, D)
    grad_value = grad_gated * gate_logistic
    grad_gate = grad_gated * value_half * gate_logistic * (1.0 - gate_logistic)
    glu_low = jnp.concatenate([grad_value, grad_gate], axis=1).astype(jnp.bfloat16)
    grad_glu_weight = left_factor(normed, glu_low)
    grad_normed = product_right(glu_low, w_glu)
    grad_input, grad_gain, grad_shift = norm_backward(
        grad_normed, unit_field, inverse, vector_full[conv_gain]
    )
    return (
        grad_field + grad_input,
        (
            grad_glu_weight,
            grad_point,
            grad_gain,
            grad_shift,
            jnp.sum(grad_value, axis=0),
            jnp.sum(grad_gate, axis=0),
            jnp.sum(grad_field, axis=0),
            local_gain,
            local_shift,
            grad_kernel,
        ),
    )


def adam_step(weight, gradient, first, second, count_steps):
    first_new = beta_first * first + (1.0 - beta_first) * gradient
    second_new = beta_second * second + (1.0 - beta_second) * gradient * gradient
    first_fix = 1.0 - jnp.power(beta_first, count_steps)
    second_fix = 1.0 - jnp.power(beta_second, count_steps)
    update = -learn_rate * (
        first_new / first_fix / (jnp.sqrt(second_new / second_fix) + adam_eps)
        + weight_decay * weight
    )
    return (first_new, second_new, update)


def shards(
    inputs,
    cotangent,
    row_weights,
    down_weights,
    hidden_bias,
    vectors,
    row_first,
    down_first,
    hidden_first,
    vector_first,
    row_second,
    down_second,
    hidden_second,
    vector_second,
    step_number,
):
    clip_count = inputs.shape[0]
    row_count = clip_count * ROWS
    shard_count = lax.axis_size("shard")
    offset_cols = 2 * FF
    hidden_cols = FF // shard_count
    vector_cols = D // shard_count
    hidden_lines = 2 * hidden_cols // vector_cols
    row_total = vectors.shape[0]

    def gather(piece):
        return lax.all_gather(piece, "shard", axis=0, tiled=True)

    w_front = gather_quarter(row_weights[:, :FF])
    down_front = gather_quarter(down_weights[0])
    small = gather_piece(
        jnp.concatenate([vectors, hidden_bias.reshape(hidden_lines, vector_cols)], axis=0)
    )
    small = small.reshape(shard_count, -1, vector_cols).astype(jnp.float32)
    vector_full = Lines(
        lax.optimization_barrier(small[:, :row_total].transpose(1, 0, 2).reshape(row_total, D))
    )
    hidden_full = Lines(
        small[:, row_total:].reshape(shard_count, 2, hidden_cols).transpose(1, 0, 2).reshape(2, FF)
    )
    w_rest = gather(row_weights[:, offset_cols:])
    w_back = gather(row_weights[:, FF:offset_cols])
    down_back = gather(down_weights[1])
    w_triple = w_rest[:, : 3 * D]
    w_place = w_rest[:, 3 * D : 4 * D]
    w_glu = w_rest[:, 4 * D : 6 * D]
    w_attend = w_rest[:, 6 * D : 7 * D]
    w_point = w_rest[:, 7 * D :]
    tables = angle_tables()
    extra = ((0, 0), (0, ROWS - CLIP_LEN), (0, 0))
    residual = jnp.pad(inputs, extra).reshape(row_count, D).astype(jnp.float32)
    cotangent_rows = jnp.pad(cotangent, extra).reshape(row_count, D)
    front, stored_leading_block = ffn_forward(
        residual, w_front, hidden_full[0], down_front, vector_full, front_gain
    )
    attended, saved_attend = attend_forward(
        front, w_triple, w_place, w_attend, vector_full, tables
    )
    convolved, saved_conv = conv_forward(attended, w_glu, w_point, vector_full)
    back_field, saved_back = ffn_forward(
        convolved, w_back, hidden_full[1], down_back, vector_full, back_gain
    )
    outputs, unit_final, inverse_final = norm_forward(
        back_field, vector_full[final_gain], vector_full[final_shift]
    )
    grad_back, final_gain_grad, final_shift_grad = norm_backward(
        cotangent_rows, unit_final, inverse_final, vector_full[final_gain]
    )
    grad_conv, back_grads = perceptron_reverse(
        grad_back, saved_back, w_back, down_back, vector_full, back_gain
    )
    grad_attended, conv_grads = conv_backward(grad_conv, saved_conv, w_glu, w_point, vector_full)
    grad_front, triple_grad, place_grad, attend_grad, attend_rows = attend_backward(
        grad_attended, saved_attend, w_triple, w_attend, vector_full, tables
    )
    grad_input, front_grads = perceptron_reverse(
        grad_front, stored_leading_block, w_front, down_front, vector_full, front_gain
    )
    hidden_grad = jnp.stack([front_grads[1], back_grads[1]])
    vector_rows = (
        [front_grads[3], front_grads[4], front_grads[5]]
        + list(attend_rows)
        + list(conv_grads[2:9])
        + [back_grads[3], back_grads[4], back_grads[5], final_gain_grad, final_shift_grad]
    )
    vector_grad = jnp.concatenate([jnp.stack(vector_rows), conv_grads[9]], axis=0)
    back_sum = reduce_piece(back_grads[0])
    down_back_sum = reduce_piece(back_grads[2])
    conv_sum = reduce_piece(jnp.concatenate([conv_grads[0], attend_grad, conv_grads[1]], axis=1))
    attend_sum = reduce_piece(jnp.concatenate([triple_grad, place_grad], axis=1))
    down_front_sum = reduce_piece(front_grads[2])
    front_sum = reduce_piece(front_grads[0])
    small_grad = jnp.concatenate(
        [
            vector_grad.reshape(row_total, shard_count, vector_cols).transpose(1, 0, 2),
            hidden_grad.reshape(2, shard_count, hidden_cols)
            .transpose(1, 0, 2)
            .reshape(shard_count, hidden_lines, vector_cols),
        ],
        axis=1,
    )
    small_sum = lax.dynamic_index_in_dim(
        sum_everywhere(small_grad), lax.axis_index("shard"), 0, keepdims=False
    )
    owned_grads = (
        jnp.concatenate([front_sum, back_sum, attend_sum, conv_sum], axis=1),
        jnp.stack([down_front_sum, down_back_sum]),
        small_sum[row_total:].reshape(2, hidden_cols),
        small_sum[:row_total],
    )
    count_steps = step_number[0].astype(jnp.float32)
    row_new = adam_step(
        row_weights.astype(jnp.float32), owned_grads[0], row_first, row_second, count_steps
    )
    down_new = adam_step(
        down_weights.astype(jnp.float32), owned_grads[1], down_first, down_second, count_steps
    )
    latent_matrix_revised = adam_step(
        hidden_bias.astype(jnp.float32), owned_grads[2], hidden_first, hidden_second, count_steps
    )
    array_revised = adam_step(
        vectors.astype(jnp.float32), owned_grads[3], vector_first, vector_second, count_steps
    )
    return (
        outputs.reshape(clip_count, ROWS, D)[:, :CLIP_LEN],
        grad_input.reshape(clip_count, ROWS, D)[:, :CLIP_LEN],
        owned_grads[0],
        owned_grads[1],
        owned_grads[2],
        owned_grads[3],
        row_new[0],
        down_new[0],
        latent_matrix_revised[0],
        array_revised[0],
        row_new[1],
        down_new[1],
        latent_matrix_revised[1],
        array_revised[1],
        row_new[2],
        down_new[2],
        latent_matrix_revised[2],
        array_revised[2],
    )


def solution(mesh):
    in_specs = (
        P(("rep", "shard"), None, None),
        P(("rep", "shard"), None, None),
        P("shard", None),
        P(None, "shard", None),
        P(None, "shard"),
        P(None, "shard"),
        P("shard", None),
        P(None, "shard", None),
        P(None, "shard"),
        P(None, "shard"),
        P("shard", None),
        P(None, "shard", None),
        P(None, "shard"),
        P(None, "shard"),
        P(),
    )
    out_specs = (
        P(("rep", "shard"), None, None),
        P(("rep", "shard"), None, None),
        P("shard", None),
        P(None, "shard", None),
        P(None, "shard"),
        P(None, "shard"),
        P("shard", None),
        P(None, "shard", None),
        P(None, "shard"),
        P(None, "shard"),
        P("shard", None),
        P(None, "shard", None),
        P(None, "shard"),
        P(None, "shard"),
        P("shard", None),
        P(None, "shard", None),
        P(None, "shard"),
        P(None, "shard"),
    )
    return jax.shard_map(shards, mesh=mesh, in_specs=in_specs, out_specs=out_specs, check_vma=False)
```
